32 devices in a mesh: grp: 4 (over y, core), dev: 8 (over z, x).
Axes of the slice: x: 2, y: 2, z: 4, core: 2. Of those that a mesh axis runs over, the one named last changes fastest.
Arguments:
- visibilities: bfloat16 [16384, 2, 128], P(('grp', 'dev')), may hold values from -6 to 6
- owner: int32 [16384, 1], P(('grp', 'dev')), may hold values from 0 to 31; in each aligned block of 512 rows (0 to 511, 512 to 1023, ...) at most 32 rows name the same one
- tile_slot: int32 [16384], P(('grp', 'dev')), may hold values from 0 to 511
- kernel_index: int32 [16384, 2], P(('grp', 'dev')), may hold values from 0 to 31
- kernels: bfloat16 [2, 32, 64, 128], replicated, may hold values from -1 to 1
Outputs:
- image: float32 [2, 8192, 8192], P(None, ('grp', 'dev'))
The draws below stay inside these ranges and needn't reach their ends.
Inputs may be any that keep to these rules, and one draw needn't show every extreme that they name: owner[r, 0] = g * 8 + d names group g and owner d; among the rows of one device no owner is named by more than 32 rows, a bound that some block reaches.
All inputs are finite; a program needn't handle non-finite values.
Results may differ from the reference program's by a relative error of at most 0.0029.
Values may be sent and summed in bfloat16 or wider, within the bound.
A program may use at most 128 MiB of HBM per device.

```python
import math
import jax
import jax.numpy as jnp
import numpy as np
from jax import lax

GRID = 8192
TILE = 64
VIS = 128
NKER = 32
ROWS_DEV = 512
ROWS = 16384
CAP = 32
TILES_DEV = 512
N_GRP = 4
N_DEV = 8


def touch_ends(entries, rng, least, high):
    shape = entries.shape
    spot = [jax.random.randint(jax.random.fold_in(rng, axis), (), 0, shape[axis]) for axis in range(len(shape))]
    entries = entries.at[tuple(spot)].set(least)
    longest = shape.index(max(shape))
    spot[longest] = (spot[longest] + 1) % shape[longest]
    return entries.at[tuple(spot)].set(high)


def block_scale(key, dims, cuts, smallest, high):
    level = 1.0
    for axis_at, blocks in cuts:
        heights = jax.random.uniform(jax.random.fold_in(jax.random.fold_in(key, 6), axis_at), (blocks,), jnp.float32, smallest / len(cuts), high / len(cuts))
        level = level * jnp.repeat(jnp.exp(heights), dims[axis_at] // blocks).reshape((-1,) + (1,) * (len(dims) - 1 - axis_at))
    return level


def assign_block(stream_key, own, number, rows, number_of, top, bound, skew):
    ranking = jax.random.permutation(stream_key, number_of)
    crowded, ordinary = shares(number_of, rows * top, bound, skew, True), shares(number_of, rows * top, bound, skew, False)
    places = jnp.arange(number_of)

    def named(lengths, rotation):
        used = int((lengths > 0).sum())
        fixed = max(1, used // 4)
        shifted = fixed + (places - fixed + rotation * (used - fixed)) % max(1, number_of - fixed)
        return jnp.zeros((number_of,), jnp.int32).at[ranking[jnp.where(places < fixed, places, shifted)]].set(jnp.asarray(lengths, jnp.int32))

    lengths = jnp.where(number % 4 == 0, named(crowded, number // 4), named(ordinary, number - number // 4 - 1))
    mixed = jax.random.permutation(jax.random.fold_in(own, 3), number_of)
    giver, taker = mixed[0:number_of // 2 * 2:2], mixed[1:number_of // 2 * 2:2]
    margin = jnp.minimum(lengths[giver] - 1, bound - lengths[taker]) // 2
    margin = jnp.where((giver == ranking[0]) | (taker == ranking[0]) | (lengths[taker] == 0), 0, jnp.maximum(margin, 0))
    shifted = jax.random.randint(jax.random.fold_in(own, 4), (number_of // 2,), 0, 1 << 20) % (margin + 1)
    lengths = lengths.at[giver].add(-shifted).at[taker].add(shifted)
    members = jnp.searchsorted(jnp.cumsum(lengths), jnp.arange(rows * top), side="right").astype(jnp.int32)
    table = members.reshape(top, rows).T
    table = table[jax.random.permutation(jax.random.fold_in(own, 1), rows)]
    rotation = jax.random.randint(jax.random.fold_in(own, 2), (rows, 1), 0, top)
    return jnp.take_along_axis(table, (jnp.arange(top)[None, :] + rotation) % top, axis=1)


def shares(count, total, most, lean, full):
    portions = [(1 << 20) // math.isqrt(rank ** lean) + 1 for rank in range(1, count + 1)]
    largest = most if full else min(most, max(-(-total // count), total * portions[0] // sum(portions)))
    least = 1 if total - largest >= count - 1 else 0
    given, surplus = [largest] + [least] * (count - 1), total - largest - least * (count - 1)
    while surplus > 0:
        movable = [i for i in range(1, count) if given[i] < largest] or [i for i in range(1, count) if given[i] < most]
        pool, remaining = sum([portions[i] for i in movable]), surplus
        for i in movable:
            addition = min(most - given[i], max(1, remaining * portions[i] // pool), surplus)
            given[i] = given[i] + addition
            surplus = surplus - addition
    return np.array(given)


def scatter_about(own_key, extent, spread, limit, split=(), held_as=jnp.bfloat16):
    values = jax.random.normal(own_key, extent, jnp.float32) * spread
    if len(split) > 0:
        values = block_scale(own_key, extent, split, -0.22, 0.18) * values
    return jnp.clip(values, min=-limit, max=limit).astype(held_as)


def setup_inputs(seed: int = 0) -> dict:
    streams_of = jax.random.split(jax.random.key(seed), 6)
    visibilities = scatter_about(streams_of[0], (ROWS, 2, VIS), 1.0, 6.0, ((0, 32),))
    owner_keys = jax.random.split(jax.random.fold_in(streams_of[1], 1), ROWS // ROWS_DEV)
    owner_turns = jax.random.permutation(jax.random.fold_in(streams_of[1], 3), ROWS // ROWS_DEV)
    owner = jax.vmap(lambda own, number: assign_block(jax.random.fold_in(streams_of[1], 2), own, number, ROWS_DEV, N_GRP * N_DEV, 1, CAP, 2))(owner_keys, owner_turns).reshape((ROWS, 1))
    tile_slot = touch_ends(jax.random.randint(streams_of[2], (ROWS,), 0, TILES_DEV), jax.random.fold_in(streams_of[2], 1), 0, TILES_DEV - 1).astype(jnp.int32)
    kernel_index = touch_ends(jax.random.randint(streams_of[3], (ROWS, 2), 0, NKER), jax.random.fold_in(streams_of[3], 1), 0, NKER - 1).astype(jnp.int32)
    kernels = scatter_about(streams_of[4], (2, NKER, TILE, VIS), 32 ** -0.5, 1.0)
    return {"visibilities": visibilities, "owner": owner, "tile_slot": tile_slot, "kernel_index": kernel_index, "kernels": kernels}


def reference(visibilities, owner, tile_slot, kernel_index, kernels):
    slab_rows = GRID // (N_GRP * N_DEV)
    tile_rows = slab_rows // TILE
    tile_cols = GRID // TILE
    per_owner = tile_rows * tile_cols
    total_rows = visibilities.shape[0]
    block_rows = 256
    block_count = total_rows // block_rows
    tile_ident = owner[:, 0].astype(jnp.int32) * per_owner + tile_slot.astype(jnp.int32)

    def grid_block(uv_tiles, block_index):
        first_row = (block_index * block_rows).astype(jnp.int32)
        vis_block = lax.dynamic_slice_in_dim(visibilities, first_row, block_rows, 0)
        kernel_block = lax.dynamic_slice_in_dim(kernel_index, first_row, block_rows, 0)
        ident_block = lax.dynamic_slice_in_dim(tile_ident, first_row, block_rows, 0)
        left_kernel = jnp.take(kernels[0], kernel_block[:, 0], axis=0).astype(jnp.float32)
        right_kernel = jnp.take(kernels[1], kernel_block[:, 1], axis=0).astype(jnp.float32)
        weighted = (left_kernel[:, None, :, :] * vis_block.astype(jnp.float32)[:, :, None, :]).astype(jnp.bfloat16)
        terms = jnp.einsum("rcik,rjk->rcij", weighted.astype(jnp.float32), right_kernel,
                           precision=lax.Precision.HIGHEST)
        return uv_tiles.at[ident_block].add(terms), None

    empty = jnp.zeros((N_GRP * N_DEV * per_owner, 2, TILE, TILE), jnp.float32)
    uv_tiles, _ = lax.scan(grid_block, empty, jnp.arange(block_count, dtype=jnp.int32))
    uv_grid = uv_tiles.reshape(N_GRP * N_DEV, tile_rows, tile_cols, 2, TILE, TILE)
    uv_grid = uv_grid.transpose(3, 0, 1, 4, 2, 5).reshape(2, GRID, GRID)
    field = lax.complex(uv_grid[0], uv_grid[1])
    result = jnp.fft.ifft2(field) * GRID
    return jnp.stack([jnp.real(result).T, jnp.imag(result).T]).astype(jnp.float32)
```

```python
import jax
import jax.numpy as jnp
import ml_dtypes
import numpy as np
from jax import lax
from jax.experimental import pallas as pl
from jax.experimental.pallas import tpu as pltpu
from jax.sharding import PartitionSpec as P

GRID = 8192
TILE = 64
VIS = 128
COARSE = GRID // TILE
GROUP = 8
STEP = 16
AXES = ("grp", "dev")


def wave(first, second, modulus):
    angle = 2.0 * np.pi / modulus * (np.outer(first, second) % modulus)
    return np.cos(angle), np.sin(angle)


def halves(table):
    high = table.astype(ml_dtypes.bfloat16)
    low = (table - high.astype(np.float64)).astype(ml_dtypes.bfloat16)
    return high, low


def tables(per_device):
    coarse, fine = np.arange(COARSE), np.arange(TILE)
    long_re, long_im = wave(coarse, coarse, COARSE)
    turn_re, turn_im = wave(coarse, fine, GRID)
    short_re, short_im = wave(fine, fine, TILE)
    row_first = halves(np.concatenate([long_re, long_im], axis=1))
    row_turn = (
        np.concatenate([turn_re, turn_re], axis=1).astype(np.float32),
        np.concatenate([-turn_im, turn_im], axis=1).astype(np.float32),
    )
    as_real = np.stack(
        [np.concatenate([short_re, -short_im], axis=1), np.concatenate([short_im, short_re], axis=1)]
    )
    as_real = as_real.reshape(2, TILE // per_device, per_device, 2 * TILE)
    high, low = halves(as_real.transpose(1, 0, 2, 3).reshape(2 * TILE, 2 * TILE))
    row_second = (np.concatenate([high, high], axis=1), low)
    col_first = halves(
        np.concatenate(
            [
                np.concatenate([long_re, long_im], axis=1),
                np.concatenate([-long_im, long_re], axis=1),
            ],
            axis=0,
        )
    )
    col_turn = (turn_re.T.astype(np.float32), turn_im.T.astype(np.float32))
    stacked = np.concatenate(
        [np.concatenate([short_re, -short_im], axis=1), np.concatenate([short_im, short_re], axis=1)],
        axis=0,
    )
    high, low = halves(stacked / GRID)
    col_second = (np.concatenate([high, high], axis=1), low)
    return row_first, row_turn, row_second, col_first, col_turn, col_second


def mm(left, right, dims=((1,), (0,))):
    return lax.dot_general(left, right, (dims, ((), ())), preferred_element_type=jnp.float32)


def split(values):
    high = values.astype(jnp.bfloat16)
    return high, (values - high.astype(jnp.float32)).astype(jnp.bfloat16)


def row_kernel(
    tile_ref, left_ref, right_ref, valid_ref, vis_ref, ka_ref, kb_ref, eh_ref, el_ref,
    wre_ref, wim_ref, fh_ref, fl_ref, out_ref, grid_ref, turn_ref,
):
    tiles = grid_ref.shape[0] // TILE
    rows = vis_ref.shape[0]

    @pl.loop(0, tiles)
    def _(tile):
        grid_ref[pl.ds(pl.multiple_of(tile * TILE, TILE), TILE), :] = jnp.zeros(
            (TILE, 2 * TILE), jnp.float32
        )

    @pl.loop(0, rows // GROUP)
    def _(group):
        first = group * GROUP

        @pl.when(valid_ref[first] > 0)
        def _():
            vis = vis_ref[pl.ds(pl.multiple_of(first, GROUP), GROUP), :]
            terms = []
            for n in range(GROUP):
                left = ka_ref[left_ref[first + n]].astype(jnp.float32)
                weighted = (left * vis[n : n + 1, :]).astype(jnp.bfloat16)
                terms.append(mm(weighted, kb_ref[right_ref[first + n]]))
            for n in range(GROUP):
                at = pl.ds(pl.multiple_of(tile_ref[first + n] * TILE, TILE), TILE)
                grid_ref[at, :] = grid_ref[at, :] + terms[n]

    lane = lax.broadcasted_iota(jnp.int32, (1, 2 * TILE), 1)
    sign = jnp.where(lane < TILE, -1.0, 1.0).astype(jnp.float32)
    span = COARSE * TILE
    pairs = 2

    @pl.loop(0, out_ref.shape[1] // STEP)
    def _(block):
        line0 = block * STEP

        @pl.loop(0, STEP // (2 * pairs))
        def _(part):
            for pair in range(pairs):
                columns = []
                for n in range(2):
                    line = line0 + part * (2 * pairs) + pair * 2 + n
                    start = (line // TILE) * span + line % TILE
                    cells = grid_ref[pl.ds(start, COARSE, stride=TILE), :]
                    swapped = pltpu.roll(cells, TILE, axis=1) * sign
                    columns.append(jnp.concatenate([cells, swapped], axis=0).astype(jnp.bfloat16))
                both = jnp.concatenate(columns, axis=1)
                middle = mm(eh_ref[...], both) + mm(el_ref[...], both)
                for n in range(2):
                    value = middle[:, n * 2 * TILE : (n + 1) * 2 * TILE]
                    value = value * wre_ref[...] + pltpu.roll(value, TILE, axis=1) * wim_ref[...]
                    high, low = split(value)
                    result = mm(
                        fh_ref[...], jnp.concatenate([high, low], axis=1), ((1,), (1,))
                    ) + mm(fl_ref[...], high, ((1,), (1,)))
                    turn_ref[
                        pl.ds(part * (2 * pairs) + pair * 2 + n, 2 * TILE, stride=STEP), :
                    ] = result

        out_ref[:, pl.ds(pl.multiple_of(line0, STEP), STEP), :] = (
            turn_ref[...].reshape(2 * TILE, STEP, COARSE).astype(jnp.bfloat16)
        )


def column_kernel(
    x_ref, eh_ref, el_ref, wre_ref, wim_ref, fh_ref, fl_ref, out_ref, wide_ref, mid_ref, turn_ref
):
    sources, lines = x_ref.shape[0], x_ref.shape[3]

    @pl.loop(0, sources)
    def _(source):
        at = pl.ds(pl.multiple_of(source * lines, lines), lines)
        for c in range(2):
            wide_ref[c, at, :] = x_ref[source, c, 0].astype(jnp.float32)

    @pl.loop(0, TILE // 2)
    def _(half):
        for n in range(2):
            i = half * 2 + n
            cells = jnp.concatenate(
                [wide_ref[c, pl.ds(i, COARSE, stride=TILE), :] for c in range(2)], axis=0
            ).astype(jnp.bfloat16)
            middle = mm(cells, eh_ref[...], ((0,), (0,))) + mm(cells, el_ref[...], ((0,), (0,)))
            re, im = middle[:, :COARSE], middle[:, COARSE:]
            wre, wim = wre_ref[pl.ds(i, 1), :], wim_ref[pl.ds(i, 1), :]
            mid_ref[0, pl.ds(i, COARSE, stride=TILE), :] = re * wre - im * wim
            mid_ref[1, pl.ds(i, COARSE, stride=TILE), :] = re * wim + im * wre

    @pl.loop(0, COARSE // 8)
    def _(block):
        for n in range(8):
            at = pl.ds(pl.multiple_of((block * 8 + n) * TILE, TILE), TILE)
            cells = jnp.concatenate([mid_ref[c, at, :] for c in range(2)], axis=0)
            high, low = split(cells)
            result = mm(fh_ref[...], jnp.concatenate([high, low], axis=0)) + mm(fl_ref[...], high)
            turn_ref[pl.ds(n, 2 * TILE, stride=8), :] = result
        rows = pl.ds(pl.multiple_of(block * 8, 8), 8)
        for c in range(2):
            for m in range(TILE):
                out_ref[c, rows, m * COARSE : (m + 1) * COARSE] = turn_ref[
                    (c * TILE + m) * 8 : (c * TILE + m + 1) * 8, :
                ]


def local(visibilities, owner, tile_slot, kernel_index, kernels):
    devices = lax.axis_size("grp") * lax.axis_size("dev")
    rows_here = visibilities.shape[0]
    capacity = 2 * rows_here // devices
    total = devices * capacity
    lines = GRID // devices
    width = GRID // devices
    blocks = max(1, width // COARSE)
    row_first, row_turn, row_second, col_first, col_turn, col_second = tables(blocks)

    target = owner[:, 0]
    onehot = target[:, None] == jnp.arange(devices, dtype=jnp.int32)[None, :]
    index = jnp.arange(rows_here, dtype=jnp.int32)
    before = (index[:, None] > index[None, :]).astype(jnp.bfloat16)
    ranks = mm(before, onehot.astype(jnp.bfloat16))
    rank = jnp.sum(jnp.where(onehot, ranks, 0.0), axis=1).astype(jnp.int32)
    position = target * capacity + rank
    place = (jnp.arange(total, dtype=jnp.int32)[:, None] == position[None, :]).astype(jnp.bfloat16)
    labels = jnp.stack(
        [
            tile_slot // COARSE,
            tile_slot % COARSE,
            kernel_index[:, 0],
            kernel_index[:, 1],
            jnp.ones_like(tile_slot),
        ],
        axis=1,
    ).astype(jnp.bfloat16)
    payload = jnp.concatenate(
        [
            visibilities.reshape(rows_here, 2 * VIS),
            jnp.pad(labels, ((0, 0), (0, VIS - labels.shape[1]))),
        ],
        axis=1,
    )
    sent = mm(place, payload).astype(jnp.bfloat16).reshape(devices, capacity, 3 * VIS)
    got = lax.all_to_all(sent, AXES, split_axis=0, concat_axis=0, tiled=True)
    got = got.reshape(total, 3 * VIS)
    vis_in = got[:, : 2 * VIS].astype(jnp.float32)
    label_in = got[:, 2 * VIS : 2 * VIS + 5].astype(jnp.int32)
    tile_in = label_in[:, 0] * COARSE + label_in[:, 1]

    left = jnp.concatenate([kernels[0], kernels[0]], axis=2)
    right = jnp.swapaxes(kernels[1], 1, 2)
    empty = jnp.zeros_like(right)
    right = jnp.concatenate(
        [jnp.concatenate([right, empty], axis=2), jnp.concatenate([empty, right], axis=2)], axis=1
    )
    smem = pl.BlockSpec(memory_space=pltpu.SMEM)
    vmem = pl.BlockSpec(memory_space=pltpu.VMEM)
    half = pl.pallas_call(
        row_kernel,
        out_shape=jax.ShapeDtypeStruct((2 * TILE, lines, COARSE), jnp.bfloat16),
        in_specs=[smem] * 4 + [vmem] * 9,
        out_specs=vmem,
        scratch_shapes=[
            pltpu.VMEM((lines * COARSE, 2 * TILE), jnp.float32),
            pltpu.VMEM((2 * TILE * STEP, COARSE), jnp.float32),
        ],
        compiler_params=pltpu.CompilerParams(vmem_limit_bytes=52 << 20),
        name="grid_rows",
    )(
        tile_in, label_in[:, 2], label_in[:, 3], label_in[:, 4], vis_in, left, right,
        *row_first, *row_turn, *row_second,
    )
    narrow = min(width, COARSE)
    if narrow < COARSE:
        parts = COARSE // narrow
        half = half.reshape(TILE, 2, lines, parts, narrow).transpose(0, 3, 1, 2, 4)
    half = half.reshape(devices, 2, blocks, lines, narrow)
    columns = lax.all_to_all(half, AXES, split_axis=0, concat_axis=0, tiled=True)
    if narrow < COARSE:
        columns = jnp.pad(columns, ((0, 0),) * 4 + ((0, COARSE - narrow),))
    fixed = lambda table: pl.BlockSpec(table.shape, lambda b: (0,) * table.ndim)
    constants = (*col_first, *col_turn, *col_second)
    image = pl.pallas_call(
        column_kernel,
        grid=(blocks,),
        out_shape=jax.ShapeDtypeStruct((2, blocks * COARSE, GRID), jnp.float32),
        in_specs=[pl.BlockSpec((devices, 2, 1, lines, COARSE), lambda b: (0, 0, b, 0, 0))]
        + [fixed(table) for table in constants],
        out_specs=pl.BlockSpec((2, COARSE, GRID), lambda b: (0, b, 0)),
        scratch_shapes=[
            pltpu.VMEM((2, GRID, COARSE), jnp.float32),
            pltpu.VMEM((2, TILE * COARSE, COARSE), jnp.float32),
            pltpu.VMEM((2 * TILE * 8, COARSE), jnp.float32),
        ],
        compiler_params=pltpu.CompilerParams(
            dimension_semantics=("arbitrary",), vmem_limit_bytes=56 << 20
        ),
        name="columns",
    )(columns, *constants)
    return image[:, :width]


def solution(mesh):
    return jax.shard_map(
        local,
        mesh=mesh,
        in_specs=(
            P(AXES, None, None),
            P(AXES, None),
            P(AXES),
            P(AXES, None),
            P(),
        ),
        out_specs=P(None, AXES, None),
        check_vma=False,
    )
```

```python
import functools

import jax
import jax.numpy as jnp
import ml_dtypes
import numpy as np
from jax import lax
from jax.experimental import pallas as pl
from jax.experimental.pallas import tpu as pltpu
from jax.sharding import PartitionSpec as P

GRID = 8192
TILE = 64
VIS = 128
COARSE = GRID // TILE
GROUP = 8
STEP = 16
AXES = ("grp", "dev")


def wave(first, second, modulus):
    angle = 2.0 * np.pi / modulus * (np.outer(first, second) % modulus)
    return np.cos(angle), np.sin(angle)


def halves(table):
    high = table.astype(ml_dtypes.bfloat16)
    low = (table - high.astype(np.float64)).astype(ml_dtypes.bfloat16)
    return high, low


def tables(per_device):
    coarse, fine = np.arange(COARSE), np.arange(TILE)
    long_re, long_im = wave(coarse, coarse, COARSE)
    turn_re, turn_im = wave(coarse, fine, GRID)
    short_re, short_im = wave(fine, fine, TILE)
    row_first = halves(np.concatenate([long_re, long_im], axis=1))
    row_turn = (
        np.concatenate([turn_re, turn_re], axis=1).astype(np.float32),
        np.concatenate([-turn_im, turn_im], axis=1).astype(np.float32),
    )
    as_real = np.stack(
        [np.concatenate([short_re, -short_im], axis=1), np.concatenate([short_im, short_re], axis=1)]
    )
    as_real = as_real.reshape(2, TILE // per_device, per_device, 2 * TILE)
    high, low = halves(as_real.transpose(1, 0, 2, 3).reshape(2 * TILE, 2 * TILE))
    row_second = (np.concatenate([high, high], axis=1), low)
    col_first = halves(
        np.concatenate(
            [
                np.concatenate([long_re, long_im], axis=1),
                np.concatenate([-long_im, long_re], axis=1),
            ],
            axis=0,
        )
    )
    col_turn = (turn_re.T.astype(np.float32), turn_im.T.astype(np.float32))
    stacked = np.concatenate(
        [np.concatenate([short_re, -short_im], axis=1), np.concatenate([short_im, short_re], axis=1)],
        axis=0,
    )
    high, low = halves(stacked / GRID)
    col_second = (np.concatenate([high, high], axis=1), low)
    return row_first, row_turn, row_second, col_first, col_turn, col_second


def mm(left, right, dims=((1,), (0,))):
    return lax.dot_general(left, right, (dims, ((), ())), preferred_element_type=jnp.float32)


def split(values):
    high = values.astype(jnp.bfloat16)
    return high, (values - high.astype(jnp.float32)).astype(jnp.bfloat16)


def grid_kernel(
    tile_ref, left_ref, right_ref, valid_ref, vis_ref, ka_ref, kb_ref, grid_ref
):
    tiles = grid_ref.shape[0] // TILE
    rows = vis_ref.shape[0]

    @pl.loop(0, tiles)
    def _(tile):
        grid_ref[pl.ds(pl.multiple_of(tile * TILE, TILE), TILE), :] = jnp.zeros(
            (TILE, 2 * TILE), jnp.float32
        )

    @pl.loop(0, rows // GROUP)
    def _(group):
        first = group * GROUP

        @pl.when(valid_ref[first] > 0)
        def _():
            vis = vis_ref[pl.ds(pl.multiple_of(first, GROUP), GROUP), :]
            terms = []
            for n in range(GROUP):
                left = ka_ref[left_ref[first + n]].astype(jnp.float32)
                weighted = (left * vis[n : n + 1, :]).astype(jnp.bfloat16)
                terms.append(mm(weighted, kb_ref[right_ref[first + n]]))
            for n in range(GROUP):
                at = pl.ds(pl.multiple_of(tile_ref[first + n] * TILE, TILE), TILE)
                grid_ref[at, :] = grid_ref[at, :] + terms[n]


def transform_block(grid_ref, tables_of, out_ref, turn_ref, line0):
    eh_ref, el_ref, wre_ref, wim_ref, fh_ref, fl_ref = tables_of
    lane = lax.broadcasted_iota(jnp.int32, (1, 2 * TILE), 1)
    sign = jnp.where(lane < TILE, -1.0, 1.0).astype(jnp.float32)
    span = COARSE * TILE
    pairs = 2

    @pl.loop(0, STEP // (2 * pairs))
    def _(part):
        for pair in range(pairs):
            columns = []
            for n in range(2):
                line = line0 + part * (2 * pairs) + pair * 2 + n
                start = (line // TILE) * span + line % TILE
                cells = grid_ref[pl.ds(start, COARSE, stride=TILE), :]
                swapped = pltpu.roll(cells, TILE, axis=1) * sign
                columns.append(jnp.concatenate([cells, swapped], axis=0).astype(jnp.bfloat16))
            both = jnp.concatenate(columns, axis=1)
            middle = mm(eh_ref[...], both) + mm(el_ref[...], both)
            for n in range(2):
                value = middle[:, n * 2 * TILE : (n + 1) * 2 * TILE]
                value = value * wre_ref[...] + pltpu.roll(value, TILE, axis=1) * wim_ref[...]
                high, low = split(value)
                result = mm(
                    fh_ref[...], jnp.concatenate([high, low], axis=1), ((1,), (1,))
                ) + mm(fl_ref[...], high, ((1,), (1,)))
                turn_ref[
                    pl.ds(part * (2 * pairs) + pair * 2 + n, 2 * TILE, stride=STEP), :
                ] = result

    out_ref[:, pl.ds(pl.multiple_of(line0, STEP), STEP), :] = (
        turn_ref[...].reshape(2 * TILE, STEP, COARSE).astype(jnp.bfloat16)
    )


def row_kernel(
    grid_ref, eh_ref, el_ref, wre_ref, wim_ref, fh_ref, fl_ref, out_ref, turn_ref
):
    tables_of = (eh_ref, el_ref, wre_ref, wim_ref, fh_ref, fl_ref)

    @pl.loop(0, out_ref.shape[1] // STEP)
    def _(block):
        transform_block(grid_ref, tables_of, out_ref, turn_ref, block * STEP)


def send_kernel(
    groups, owners, grid_ref, eh_ref, el_ref, wre_ref, wim_ref, fh_ref, fl_ref, got_ref,
    stage_ref, turn_ref, send_sem, recv_sem, own_sem,
):
    tables_of = (eh_ref, el_ref, wre_ref, wim_ref, fh_ref, fl_ref)
    devices = groups * owners
    strips = stage_ref.shape[1] // TILE
    share = stage_ref.shape[0] // devices
    me = lax.axis_index("grp") * owners + lax.axis_index("dev")

    def piece(strip, peer):
        rows = pl.ds(strip * TILE, TILE)
        return pltpu.make_async_remote_copy(
            src_ref=stage_ref.at[pl.ds(peer * share, share), rows, :],
            dst_ref=got_ref.at[me, :, rows, :],
            send_sem=send_sem.at[strip, peer],
            recv_sem=recv_sem.at[strip, me],
            device_id=(peer // owners, peer % owners),
            device_id_type=pl.DeviceIdType.MESH,
        )

    def arrival(strip, peer):
        rows = pl.ds(strip * TILE, TILE)
        return pltpu.make_async_remote_copy(
            src_ref=stage_ref.at[pl.ds(peer * share, share), rows, :],
            dst_ref=got_ref.at[peer, :, rows, :],
            send_sem=send_sem.at[strip, peer],
            recv_sem=recv_sem.at[strip, peer],
            device_id=(peer // owners, peer % owners),
            device_id_type=pl.DeviceIdType.MESH,
        )

    own = pltpu.make_async_copy(
        stage_ref.at[pl.ds(me * share, share), :, :], got_ref.at[me], own_sem
    )
    for strip in range(strips):
        @pl.loop(0, TILE // STEP)
        def _(block):
            transform_block(grid_ref, tables_of, stage_ref, turn_ref, strip * TILE + block * STEP)

        @pl.loop(1, devices)
        def _(n):
            piece(strip, (me + n) % devices).start()

    own.start()
    own.wait()
    for strip in range(strips):
        @pl.loop(1, devices)
        def _(n):
            piece(strip, (me + n) % devices).wait_send()

        @pl.loop(1, devices)
        def _(n):
            arrival(strip, (me + n) % devices).wait_recv()


def column_kernel(
    x_ref, eh_ref, el_ref, wre_ref, wim_ref, fh_ref, fl_ref, out_ref, wide_ref, mid_ref, turn_ref
):
    sources, lines = x_ref.shape[0], x_ref.shape[3]

    @pl.loop(0, sources)
    def _(source):
        at = pl.ds(pl.multiple_of(source * lines, lines), lines)
        for c in range(2):
            wide_ref[c, at, :] = x_ref[source, c, 0].astype(jnp.float32)

    @pl.loop(0, TILE // 2)
    def _(half):
        for n in range(2):
            i = half * 2 + n
            cells = jnp.concatenate(
                [wide_ref[c, pl.ds(i, COARSE, stride=TILE), :] for c in range(2)], axis=0
            ).astype(jnp.bfloat16)
            middle = mm(cells, eh_ref[...], ((0,), (0,))) + mm(cells, el_ref[...], ((0,), (0,)))
            re, im = middle[:, :COARSE], middle[:, COARSE:]
            wre, wim = wre_ref[pl.ds(i, 1), :], wim_ref[pl.ds(i, 1), :]
            mid_ref[0, pl.ds(i, COARSE, stride=TILE), :] = re * wre - im * wim
            mid_ref[1, pl.ds(i, COARSE, stride=TILE), :] = re * wim + im * wre

    @pl.loop(0, COARSE // 8)
    def _(block):
        for n in range(8):
            at = pl.ds(pl.multiple_of((block * 8 + n) * TILE, TILE), TILE)
            cells = jnp.concatenate([mid_ref[c, at, :] for c in range(2)], axis=0)
            high, low = split(cells)
            result = mm(fh_ref[...], jnp.concatenate([high, low], axis=0)) + mm(fl_ref[...], high)
            turn_ref[pl.ds(n, 2 * TILE, stride=8), :] = result
        rows = pl.ds(pl.multiple_of(block * 8, 8), 8)
        for c in range(2):
            for m in range(TILE):
                out_ref[c, rows, m * COARSE : (m + 1) * COARSE] = turn_ref[
                    (c * TILE + m) * 8 : (c * TILE + m + 1) * 8, :
                ]


def local(visibilities, owner, tile_slot, kernel_index, kernels):
    devices = lax.axis_size("grp") * lax.axis_size("dev")
    rows_here = visibilities.shape[0]
    capacity = 2 * rows_here // devices
    total = devices * capacity
    lines = GRID // devices
    width = GRID // devices
    blocks = max(1, width // COARSE)
    row_first, row_turn, row_second, col_first, col_turn, col_second = tables(blocks)

    target = owner[:, 0]
    onehot = target[:, None] == jnp.arange(devices, dtype=jnp.int32)[None, :]
    index = jnp.arange(rows_here, dtype=jnp.int32)
    before = (index[:, None] > index[None, :]).astype(jnp.bfloat16)
    ranks = mm(before, onehot.astype(jnp.bfloat16))
    rank = jnp.sum(jnp.where(onehot, ranks, 0.0), axis=1).astype(jnp.int32)
    position = target * capacity + rank
    place = (jnp.arange(total, dtype=jnp.int32)[:, None] == position[None, :]).astype(jnp.bfloat16)
    labels = jnp.stack(
        [
            tile_slot // COARSE,
            tile_slot % COARSE,
            kernel_index[:, 0],
            kernel_index[:, 1],
            jnp.ones_like(tile_slot),
        ],
        axis=1,
    ).astype(jnp.bfloat16)
    payload = jnp.concatenate(
        [
            visibilities.reshape(rows_here, 2 * VIS),
            jnp.pad(labels, ((0, 0), (0, VIS - labels.shape[1]))),
        ],
        axis=1,
    )
    sent = mm(place, payload).astype(jnp.bfloat16).reshape(devices, capacity, 3 * VIS)
    got = lax.all_to_all(sent, AXES, split_axis=0, concat_axis=0, tiled=True)
    got = got.reshape(total, 3 * VIS)
    vis_in = got[:, : 2 * VIS].astype(jnp.float32)
    label_in = got[:, 2 * VIS : 2 * VIS + 5].astype(jnp.int32)
    tile_in = label_in[:, 0] * COARSE + label_in[:, 1]

    left = jnp.concatenate([kernels[0], kernels[0]], axis=2)
    right = jnp.swapaxes(kernels[1], 1, 2)
    empty = jnp.zeros_like(right)
    right = jnp.concatenate(
        [jnp.concatenate([right, empty], axis=2), jnp.concatenate([empty, right], axis=2)], axis=1
    )
    smem = pl.BlockSpec(memory_space=pltpu.SMEM)
    vmem = pl.BlockSpec(memory_space=pltpu.VMEM)
    field = pl.pallas_call(
        grid_kernel,
        out_shape=jax.ShapeDtypeStruct((lines * COARSE, 2 * TILE), jnp.float32),
        in_specs=[smem] * 4 + [vmem] * 3,
        out_specs=vmem,
        compiler_params=pltpu.CompilerParams(vmem_limit_bytes=40 << 20),
        name="grid_cells",
    )(tile_in, label_in[:, 2], label_in[:, 3], label_in[:, 4], vis_in, left, right)
    row_tables = (*row_first, *row_turn, *row_second)
    turned = pltpu.VMEM((2 * TILE * STEP, COARSE), jnp.float32)
    if width >= COARSE:
        columns = pl.pallas_call(
            functools.partial(send_kernel, lax.axis_size("grp"), lax.axis_size("dev")),
            out_shape=jax.ShapeDtypeStruct((devices, 2 * blocks, lines, COARSE), jnp.bfloat16),
            in_specs=[vmem] * 7,
            out_specs=pl.BlockSpec(memory_space=pl.ANY),
            scratch_shapes=[
                pltpu.VMEM((2 * TILE, lines, COARSE), jnp.bfloat16),
                turned,
                pltpu.SemaphoreType.DMA((lines // TILE, devices)),
                pltpu.SemaphoreType.DMA((lines // TILE, devices)),
                pltpu.SemaphoreType.DMA,
            ],
            compiler_params=pltpu.CompilerParams(
                vmem_limit_bytes=52 << 20, has_side_effects=True
            ),
            name="rows_sent",
        )(field, *row_tables)
        columns = columns.reshape(devices, 2, blocks, lines, COARSE)
    else:
        half = pl.pallas_call(
            row_kernel,
            out_shape=jax.ShapeDtypeStruct((2 * TILE, lines, COARSE), jnp.bfloat16),
            in_specs=[vmem] * 7,
            out_specs=vmem,
            scratch_shapes=[turned],
            compiler_params=pltpu.CompilerParams(vmem_limit_bytes=52 << 20),
            name="rows",
        )(field, *row_tables)
        parts = COARSE // width
        half = half.reshape(TILE, 2, lines, parts, width).transpose(0, 3, 1, 2, 4)
        half = half.reshape(devices, 2, blocks, lines, width)
        columns = lax.all_to_all(half, AXES, split_axis=0, concat_axis=0, tiled=True)
        columns = jnp.pad(columns, ((0, 0),) * 4 + ((0, COARSE - width),))
    fixed = lambda table: pl.BlockSpec(table.shape, lambda b: (0,) * table.ndim)
    constants = (*col_first, *col_turn, *col_second)
    image = pl.pallas_call(
        column_kernel,
        grid=(blocks,),
        out_shape=jax.ShapeDtypeStruct((2, blocks * COARSE, GRID), jnp.float32),
        in_specs=[pl.BlockSpec((devices, 2, 1, lines, COARSE), lambda b: (0, 0, b, 0, 0))]
        + [fixed(table) for table in constants],
        out_specs=pl.BlockSpec((2, COARSE, GRID), lambda b: (0, b, 0)),
        scratch_shapes=[
            pltpu.VMEM((2, GRID, COARSE), jnp.float32),
            pltpu.VMEM((2, TILE * COARSE, COARSE), jnp.float32),
            pltpu.VMEM((2 * TILE * 8, COARSE), jnp.float32),
        ],
        compiler_params=pltpu.CompilerParams(
            dimension_semantics=("arbitrary",), vmem_limit_bytes=56 << 20
        ),
        name="columns",
    )(columns, *constants)
    return image[:, :width]


def solution(mesh):
    return jax.shard_map(
        local,
        mesh=mesh,
        in_specs=(
            P(AXES, None, None),
            P(AXES, None),
            P(AXES),
            P(AXES, None),
            P(),
        ),
        out_specs=P(None, AXES, None),
        check_vma=False,
    )
```

```python
import functools

import jax
import jax.numpy as jnp
import ml_dtypes
import numpy as np
from jax import lax
from jax.experimental import pallas as pl
from jax.experimental.pallas import tpu as pltpu
from jax.sharding import PartitionSpec as P

GRID = 8192
TILE = 64
VIS = 128
COARSE = GRID // TILE
GROUP = 8
STEP = 16
AXES = ("grp", "dev")


def wave(first, second, modulus):
    angle = 2.0 * np.pi / modulus * (np.outer(first, second) % modulus)
    return np.cos(angle), np.sin(angle)


def halves(table):
    high = table.astype(ml_dtypes.bfloat16)
    low = (table - high.astype(np.float64)).astype(ml_dtypes.bfloat16)
    return high, low


def tables(per_device):
    coarse, fine = np.arange(COARSE), np.arange(TILE)
    long_re, long_im = wave(coarse, coarse, COARSE)
    turn_re, turn_im = wave(coarse, fine, GRID)
    short_re, short_im = wave(fine, fine, TILE)
    row_first = halves(np.concatenate([long_re, long_im], axis=1))
    row_turn = (
        np.concatenate([turn_re, turn_re], axis=1).astype(np.float32),
        np.concatenate([-turn_im, turn_im], axis=1).astype(np.float32),
    )
    as_real = np.stack(
        [np.concatenate([short_re, -short_im], axis=1), np.concatenate([short_im, short_re], axis=1)]
    )
    as_real = as_real.reshape(2, TILE // per_device, per_device, 2 * TILE)
    high, low = halves(as_real.transpose(1, 0, 2, 3).reshape(2 * TILE, 2 * TILE))
    row_second = (np.concatenate([high, high], axis=1), low)
    col_first = halves(
        np.concatenate(
            [
                np.concatenate([long_re, long_im], axis=1),
                np.concatenate([-long_im, long_re], axis=1),
            ],
            axis=0,
        )
    )
    col_turn = (turn_re.T.astype(np.float32), turn_im.T.astype(np.float32))
    stacked = np.concatenate(
        [np.concatenate([short_re, -short_im], axis=1), np.concatenate([short_im, short_re], axis=1)],
        axis=0,
    )
    high, low = halves(stacked / GRID)
    col_second = (np.concatenate([high, high], axis=1), low)
    return row_first, row_turn, row_second, col_first, col_turn, col_second


def mm(left, right, dims=((1,), (0,))):
    return lax.dot_general(left, right, (dims, ((), ())), preferred_element_type=jnp.float32)


def split(values):
    high = values.astype(jnp.bfloat16)
    return high, (values - high.astype(jnp.float32)).astype(jnp.bfloat16)


def grid_kernel(
    tile_ref, left_ref, right_ref, valid_ref, vis_ref, ka_ref, kb_ref, grid_ref
):
    tiles = grid_ref.shape[0] // TILE
    rows = vis_ref.shape[0]

    @pl.loop(0, tiles)
    def _(tile):
        grid_ref[pl.ds(pl.multiple_of(tile * TILE, TILE), TILE), :] = jnp.zeros(
            (TILE, 2 * TILE), jnp.float32
        )

    @pl.loop(0, rows // GROUP)
    def _(group):
        first = group * GROUP

        @pl.when(valid_ref[first] > 0)
        def _():
            vis = vis_ref[pl.ds(pl.multiple_of(first, GROUP), GROUP), :]
            terms = []
            for n in range(GROUP):
                left = ka_ref[left_ref[first + n]].astype(jnp.float32)
                weighted = (left * vis[n : n + 1, :]).astype(jnp.bfloat16)
                terms.append(mm(weighted, kb_ref[right_ref[first + n]]))
            for n in range(GROUP):
                at = pl.ds(pl.multiple_of(tile_ref[first + n] * TILE, TILE), TILE)
                grid_ref[at, :] = grid_ref[at, :] + terms[n]


def transform_block(grid_ref, tables_of, out_ref, turn_ref, line0):
    eh_ref, el_ref, wre_ref, wim_ref, fh_ref, fl_ref = tables_of
    lane = lax.broadcasted_iota(jnp.int32, (1, 2 * TILE), 1)
    sign = jnp.where(lane < TILE, -1.0, 1.0).astype(jnp.float32)
    span = COARSE * TILE
    pairs = 2
    shares = fh_ref.shape[0]

    @pl.loop(0, STEP // (2 * pairs))
    def _(part):
        for pair in range(pairs):
            columns = []
            for n in range(2):
                line = line0 + part * (2 * pairs) + pair * 2 + n
                start = (line // TILE) * span + line % TILE
                cells = grid_ref[pl.ds(start, COARSE, stride=TILE), :]
                swapped = pltpu.roll(cells, TILE, axis=1) * sign
                columns.append(jnp.concatenate([cells, swapped], axis=0).astype(jnp.bfloat16))
            both = jnp.concatenate(columns, axis=1)
            middle = mm(eh_ref[...], both) + mm(el_ref[...], both)
            for n in range(2):
                value = middle[:, n * 2 * TILE : (n + 1) * 2 * TILE]
                value = value * wre_ref[...] + pltpu.roll(value, TILE, axis=1) * wim_ref[...]
                high, low = split(value)
                result = mm(
                    fh_ref[...], jnp.concatenate([high, low], axis=1), ((1,), (1,))
                ) + mm(fl_ref[...], high, ((1,), (1,)))
                turn_ref[
                    pl.ds(part * (2 * pairs) + pair * 2 + n, shares, stride=STEP), :
                ] = result

    out_ref[:, pl.ds(pl.multiple_of(line0, STEP), STEP), :] = (
        turn_ref[...].reshape(shares, STEP, COARSE).astype(jnp.bfloat16)
    )


def row_kernel(
    grid_ref, eh_ref, el_ref, wre_ref, wim_ref, fh_ref, fl_ref, out_ref, turn_ref
):
    tables_of = (eh_ref, el_ref, wre_ref, wim_ref, fh_ref, fl_ref)

    @pl.loop(0, out_ref.shape[1] // STEP)
    def _(block):
        transform_block(grid_ref, tables_of, out_ref, turn_ref, block * STEP)


def send_kernel(
    groups, owners, grid_ref, eh_ref, el_ref, wre_ref, wim_ref, fh_ref, fl_ref, got_ref,
    stage_ref, turn_ref, send_sem, recv_sem, own_sem,
):
    tables_of = (eh_ref, el_ref, wre_ref, wim_ref, fh_ref, fl_ref)
    near = owners // 2
    peers = groups * near
    strips = stage_ref.shape[1] // TILE
    per_owner = got_ref.shape[2] // TILE
    share = stage_ref.shape[0] // peers
    group, place = lax.axis_index("grp"), lax.axis_index("dev")
    side = place // near
    mine = group * near + place % near

    def owner_of(peer, strip):
        at = side if strip < per_owner else 1 - side
        return (peer // near) * owners + at * near + peer % near

    def piece(strip, peer, source):
        return pltpu.make_async_remote_copy(
            src_ref=stage_ref.at[pl.ds(peer * share, share), pl.ds(strip * TILE, TILE), :],
            dst_ref=got_ref.at[
                owner_of(source, strip), :, pl.ds(strip % per_owner * TILE, TILE), :
            ],
            send_sem=send_sem.at[strip, peer],
            recv_sem=recv_sem.at[strip, source],
            device_id=(peer // near, side * near + peer % near),
            device_id_type=pl.DeviceIdType.MESH,
        )

    for strip in range(strips):
        @pl.loop(0, TILE // STEP)
        def _(block):
            transform_block(grid_ref, tables_of, stage_ref, turn_ref, strip * TILE + block * STEP)

        @pl.loop(1, peers)
        def _(n):
            piece(strip, (mine + n) % peers, mine).start()

    lines = per_owner * TILE
    for part in range(2):
        own = pltpu.make_async_copy(
            stage_ref.at[pl.ds(mine * share, share), pl.ds(part * lines, lines), :],
            got_ref.at[owner_of(mine, part * per_owner)],
            own_sem.at[part],
        )
        own.start()
        own.wait()
    for strip in range(strips):
        @pl.loop(1, peers)
        def _(n):
            piece(strip, (mine + n) % peers, mine).wait_send()

        @pl.loop(1, peers)
        def _(n):
            peer = (mine + n) % peers
            piece(strip, peer, peer).wait_recv()


def column_kernel(
    x_ref, eh_ref, el_ref, wre_ref, wim_ref, fh_ref, fl_ref, out_ref, wide_ref, mid_ref, turn_ref
):
    sources, lines = x_ref.shape[0], x_ref.shape[3]

    @pl.loop(0, sources)
    def _(source):
        at = pl.ds(pl.multiple_of(source * lines, lines), lines)
        for c in range(2):
            wide_ref[c, at, :] = x_ref[source, c, 0].astype(jnp.float32)

    @pl.loop(0, TILE // 2)
    def _(half):
        for n in range(2):
            i = half * 2 + n
            cells = jnp.concatenate(
                [wide_ref[c, pl.ds(i, COARSE, stride=TILE), :] for c in range(2)], axis=0
            ).astype(jnp.bfloat16)
            middle = mm(cells, eh_ref[...], ((0,), (0,))) + mm(cells, el_ref[...], ((0,), (0,)))
            re, im = middle[:, :COARSE], middle[:, COARSE:]
            wre, wim = wre_ref[pl.ds(i, 1), :], wim_ref[pl.ds(i, 1), :]
            mid_ref[0, pl.ds(i, COARSE, stride=TILE), :] = re * wre - im * wim
            mid_ref[1, pl.ds(i, COARSE, stride=TILE), :] = re * wim + im * wre

    @pl.loop(0, COARSE // 8)
    def _(block):
        for n in range(8):
            at = pl.ds(pl.multiple_of((block * 8 + n) * TILE, TILE), TILE)
            cells = jnp.concatenate([mid_ref[c, at, :] for c in range(2)], axis=0)
            high, low = split(cells)
            result = mm(fh_ref[...], jnp.concatenate([high, low], axis=0)) + mm(fl_ref[...], high)
            turn_ref[pl.ds(n, 2 * TILE, stride=8), :] = result
        rows = pl.ds(pl.multiple_of(block * 8, 8), 8)
        for c in range(2):
            for m in range(TILE):
                out_ref[c, rows, m * COARSE : (m + 1) * COARSE] = turn_ref[
                    (c * TILE + m) * 8 : (c * TILE + m + 1) * 8, :
                ]


def local(visibilities, owner, tile_slot, kernel_index, kernels):
    devices = lax.axis_size("grp") * lax.axis_size("dev")
    rows_here = visibilities.shape[0]
    capacity = 2 * rows_here // devices
    total = devices * capacity
    lines = GRID // devices
    width = GRID // devices
    blocks = max(1, width // COARSE)
    row_first, row_turn, row_second, col_first, col_turn, col_second = tables(blocks)

    target = owner[:, 0]
    onehot = target[:, None] == jnp.arange(devices, dtype=jnp.int32)[None, :]
    index = jnp.arange(rows_here, dtype=jnp.int32)
    before = (index[:, None] > index[None, :]).astype(jnp.bfloat16)
    ranks = mm(before, onehot.astype(jnp.bfloat16))
    rank = jnp.sum(jnp.where(onehot, ranks, 0.0), axis=1).astype(jnp.int32)
    position = target * capacity + rank
    place = (jnp.arange(total, dtype=jnp.int32)[:, None] == position[None, :]).astype(jnp.bfloat16)
    labels = jnp.stack(
        [
            tile_slot // COARSE,
            tile_slot % COARSE,
            kernel_index[:, 0],
            kernel_index[:, 1],
            jnp.ones_like(tile_slot),
        ],
        axis=1,
    ).astype(jnp.bfloat16)
    payload = jnp.concatenate(
        [
            visibilities.reshape(rows_here, 2 * VIS),
            jnp.pad(labels, ((0, 0), (0, VIS - labels.shape[1]))),
        ],
        axis=1,
    )
    sent = mm(place, payload).astype(jnp.bfloat16).reshape(devices, capacity, 3 * VIS)
    groups, owners = lax.axis_size("grp"), lax.axis_size("dev")
    copies = 2 if width >= COARSE else 1
    if copies == 2:
        other = sent.reshape(groups, 2, owners // 2, capacity, 3 * VIS)[:, ::-1]
        sent = jnp.concatenate([sent, other.reshape(sent.shape)], axis=1)
    got = lax.all_to_all(sent, AXES, split_axis=0, concat_axis=0, tiled=True)
    total = copies * total
    got = got.reshape(total, 3 * VIS)
    vis_in = got[:, : 2 * VIS].astype(jnp.float32)
    label_in = got[:, 2 * VIS : 2 * VIS + 5].astype(jnp.int32)
    part = jnp.arange(total, dtype=jnp.int32) // capacity % copies
    tile_in = (part * (lines // TILE) + label_in[:, 0]) * COARSE + label_in[:, 1]

    left = jnp.concatenate([kernels[0], kernels[0]], axis=2)
    right = jnp.swapaxes(kernels[1], 1, 2)
    empty = jnp.zeros_like(right)
    right = jnp.concatenate(
        [jnp.concatenate([right, empty], axis=2), jnp.concatenate([empty, right], axis=2)], axis=1
    )
    smem = pl.BlockSpec(memory_space=pltpu.SMEM)
    vmem = pl.BlockSpec(memory_space=pltpu.VMEM)
    field = pl.pallas_call(
        grid_kernel,
        out_shape=jax.ShapeDtypeStruct((copies * lines * COARSE, 2 * TILE), jnp.float32),
        in_specs=[smem] * 4 + [vmem] * 3,
        out_specs=vmem,
        compiler_params=pltpu.CompilerParams(vmem_limit_bytes=48 << 20),
        name="grid_cells",
    )(tile_in, label_in[:, 2], label_in[:, 3], label_in[:, 4], vis_in, left, right)
    shares = 2 * TILE // copies
    if copies == 2:
        side = lax.axis_index("dev") // (owners // 2)
        row_second = [
            lax.dynamic_index_in_dim(
                jnp.asarray(table).reshape(groups, 2, shares // groups, table.shape[1]),
                side, 1, keepdims=False,
            ).reshape(shares, table.shape[1])
            for table in row_second
        ]
    row_tables = (*row_first, *row_turn, *row_second)
    turned = pltpu.VMEM((shares * STEP, COARSE), jnp.float32)
    if copies == 2:
        columns = pl.pallas_call(
            functools.partial(send_kernel, groups, owners),
            out_shape=jax.ShapeDtypeStruct((devices, 2 * blocks, lines, COARSE), jnp.bfloat16),
            in_specs=[vmem] * 7,
            out_specs=pl.BlockSpec(memory_space=pl.ANY),
            scratch_shapes=[
                pltpu.VMEM((shares, copies * lines, COARSE), jnp.bfloat16),
                turned,
                pltpu.SemaphoreType.DMA((copies * lines // TILE, devices // copies)),
                pltpu.SemaphoreType.DMA((copies * lines // TILE, devices // copies)),
                pltpu.SemaphoreType.DMA((2,)),
            ],
            compiler_params=pltpu.CompilerParams(
                vmem_limit_bytes=54 << 20, has_side_effects=True
            ),
            name="rows_sent",
        )(field, *row_tables)
        columns = columns.reshape(devices, 2, blocks, lines, COARSE)
    else:
        half = pl.pallas_call(
            row_kernel,
            out_shape=jax.ShapeDtypeStruct((2 * TILE, lines, COARSE), jnp.bfloat16),
            in_specs=[vmem] * 7,
            out_specs=vmem,
            scratch_shapes=[turned],
            compiler_params=pltpu.CompilerParams(vmem_limit_bytes=52 << 20),
            name="rows",
        )(field, *row_tables)
        parts = COARSE // width
        half = half.reshape(TILE, 2, lines, parts, width).transpose(0, 3, 1, 2, 4)
        half = half.reshape(devices, 2, blocks, lines, width)
        columns = lax.all_to_all(half, AXES, split_axis=0, concat_axis=0, tiled=True)
        columns = jnp.pad(columns, ((0, 0),) * 4 + ((0, COARSE - width),))
    fixed = lambda table: pl.BlockSpec(table.shape, lambda b: (0,) * table.ndim)
    constants = (*col_first, *col_turn, *col_second)
    image = pl.pallas_call(
        column_kernel,
        grid=(blocks,),
        out_shape=jax.ShapeDtypeStruct((2, blocks * COARSE, GRID), jnp.float32),
        in_specs=[pl.BlockSpec((devices, 2, 1, lines, COARSE), lambda b: (0, 0, b, 0, 0))]
        + [fixed(table) for table in constants],
        out_specs=pl.BlockSpec((2, COARSE, GRID), lambda b: (0, b, 0)),
        scratch_shapes=[
            pltpu.VMEM((2, GRID, COARSE), jnp.float32),
            pltpu.VMEM((2, TILE * COARSE, COARSE), jnp.float32),
            pltpu.VMEM((2 * TILE * 8, COARSE), jnp.float32),
        ],
        compiler_params=pltpu.CompilerParams(
            dimension_semantics=("arbitrary",), vmem_limit_bytes=56 << 20
        ),
        name="columns",
    )(columns, *constants)
    return image[:, :width]


def solution(mesh):
    return jax.shard_map(
        local,
        mesh=mesh,
        in_specs=(
            P(AXES, None, None),
            P(AXES, None),
            P(AXES),
            P(AXES, None),
            P(),
        ),
        out_specs=P(None, AXES, None),
        check_vma=False,
    )
```

```python
import functools

import jax
import jax.numpy as jnp
import ml_dtypes
import numpy as np
from jax import lax
from jax.experimental import pallas as pl
from jax.experimental.pallas import tpu as pltpu
from jax.sharding import PartitionSpec as P

GRID = 8192
TILE = 64
VIS = 128
COARSE = GRID // TILE
GROUP = 8
STEP = 16
AXES = ("grp", "dev")


def wave(first, second, modulus):
    angle = 2.0 * np.pi / modulus * (np.outer(first, second) % modulus)
    return np.cos(angle), np.sin(angle)


def halves(table):
    high = table.astype(ml_dtypes.bfloat16)
    low = (table - high.astype(np.float64)).astype(ml_dtypes.bfloat16)
    return high, low


def tables(per_device):
    coarse, fine = np.arange(COARSE), np.arange(TILE)
    long_re, long_im = wave(coarse, coarse, COARSE)
    turn_re, turn_im = wave(coarse, fine, GRID)
    short_re, short_im = wave(fine, fine, TILE)
    row_first = halves(np.concatenate([long_re, long_im], axis=1))
    row_turn = (
        np.concatenate([turn_re, turn_re], axis=1).astype(np.float32),
        np.concatenate([-turn_im, turn_im], axis=1).astype(np.float32),
    )
    as_real = np.stack(
        [np.concatenate([short_re, -short_im], axis=1), np.concatenate([short_im, short_re], axis=1)]
    )
    as_real = as_real.reshape(2, TILE // per_device, per_device, 2 * TILE)
    high, low = halves(as_real.transpose(1, 0, 2, 3).reshape(2 * TILE, 2 * TILE))
    row_second = (
        np.concatenate([high, high], axis=1),
        np.concatenate([low, np.zeros_like(low)], axis=1),
    )
    col_first = halves(
        np.concatenate(
            [
                np.concatenate([long_re, long_im], axis=1),
                np.concatenate([-long_im, long_re], axis=1),
            ],
            axis=0,
        )
    )
    col_turn = (turn_re.T.astype(np.float32), turn_im.T.astype(np.float32))
    stacked = np.concatenate(
        [np.concatenate([short_re, -short_im], axis=1), np.concatenate([short_im, short_re], axis=1)],
        axis=0,
    )
    high, low = halves(stacked / GRID)
    col_second = (
        np.concatenate([high, high], axis=1),
        np.concatenate([low, np.zeros_like(low)], axis=1),
    )
    return row_first, row_turn, row_second, col_first, col_turn, col_second


def mm(left, right, dims=((1,), (0,))):
    return lax.dot_general(left, right, (dims, ((), ())), preferred_element_type=jnp.float32)


def split(values):
    high = values.astype(jnp.bfloat16)
    return high, (values - high.astype(jnp.float32)).astype(jnp.bfloat16)


def grid_kernel(
    tile_ref, left_ref, right_ref, valid_ref, vis_ref, ka_ref, kb_ref, grid_ref
):
    tiles = grid_ref.shape[0] // TILE
    rows = vis_ref.shape[0]

    @pl.loop(0, tiles)
    def _(tile):
        grid_ref[pl.ds(pl.multiple_of(tile * TILE, TILE), TILE), :] = jnp.zeros(
            (TILE, 2 * TILE), jnp.float32
        )

    @pl.loop(0, rows // GROUP)
    def _(group):
        first = group * GROUP

        @pl.when(valid_ref[first] > 0)
        def _():
            vis = vis_ref[pl.ds(pl.multiple_of(first, GROUP), GROUP), :]
            terms = []
            for n in range(GROUP):
                left = ka_ref[left_ref[first + n]].astype(jnp.float32)
                weighted = (left * vis[n : n + 1, :]).astype(jnp.bfloat16)
                terms.append(mm(weighted, kb_ref[right_ref[first + n]]))
            for n in range(GROUP):
                at = pl.ds(pl.multiple_of(tile_ref[first + n] * TILE, TILE), TILE)
                grid_ref[at, :] = grid_ref[at, :] + terms[n]


def transform_block(grid_ref, tables_of, out_ref, turn_ref, line0):
    eh_ref, el_ref, wre_ref, wim_ref, fh_ref, fl_ref = tables_of
    lane = lax.broadcasted_iota(jnp.int32, (1, 2 * TILE), 1)
    sign = jnp.where(lane < TILE, -1.0, 1.0).astype(jnp.float32)
    span = COARSE * TILE
    pairs = 2
    shares = fh_ref.shape[0]

    @pl.loop(0, STEP // (2 * pairs))
    def _(part):
        for pair in range(pairs):
            columns = []
            for n in range(2):
                line = line0 + part * (2 * pairs) + pair * 2 + n
                start = (line // TILE) * span + line % TILE
                cells = grid_ref[pl.ds(start, COARSE, stride=TILE), :]
                swapped = pltpu.roll(cells, TILE, axis=1) * sign
                columns.append(jnp.concatenate([cells, swapped], axis=0).astype(jnp.bfloat16))
            both = jnp.concatenate(columns, axis=1)
            middle = mm(jnp.concatenate([eh_ref[...], el_ref[...]], axis=0), both)
            middle = middle[:COARSE] + middle[COARSE:]
            for n in range(2):
                value = middle[:, n * 2 * TILE : (n + 1) * 2 * TILE]
                value = value * wre_ref[...] + pltpu.roll(value, TILE, axis=1) * wim_ref[...]
                high, low = split(value)
                result = mm(
                    jnp.concatenate([fh_ref[...], fl_ref[...]], axis=0),
                    jnp.concatenate([high, low], axis=1),
                    ((1,), (1,)),
                )
                result = result[:shares] + result[shares:]
                turn_ref[
                    pl.ds(part * (2 * pairs) + pair * 2 + n, shares, stride=STEP), :
                ] = result

    out_ref[:, pl.ds(pl.multiple_of(line0, STEP), STEP), :] = (
        turn_ref[...].reshape(shares, STEP, COARSE).astype(jnp.bfloat16)
    )


def row_kernel(
    grid_ref, eh_ref, el_ref, wre_ref, wim_ref, fh_ref, fl_ref, out_ref, turn_ref
):
    tables_of = (eh_ref, el_ref, wre_ref, wim_ref, fh_ref, fl_ref)

    @pl.loop(0, out_ref.shape[1] // STEP)
    def _(block):
        transform_block(grid_ref, tables_of, out_ref, turn_ref, block * STEP)


def send_kernel(
    groups, owners, grid_ref, eh_ref, el_ref, wre_ref, wim_ref, fh_ref, fl_ref, got_ref,
    stage_ref, turn_ref, send_sem, recv_sem, own_sem,
):
    tables_of = (eh_ref, el_ref, wre_ref, wim_ref, fh_ref, fl_ref)
    near = owners // 2
    peers = groups * near
    strips = stage_ref.shape[1] // TILE
    per_owner = got_ref.shape[2] // TILE
    share = stage_ref.shape[0] // peers
    group, place = lax.axis_index("grp"), lax.axis_index("dev")
    side = place // near
    mine = group * near + place % near

    def owner_of(peer, strip):
        at = side if strip < per_owner else 1 - side
        return (peer // near) * owners + at * near + peer % near

    def piece(strip, peer, source):
        return pltpu.make_async_remote_copy(
            src_ref=stage_ref.at[pl.ds(peer * share, share), pl.ds(strip * TILE, TILE), :],
            dst_ref=got_ref.at[
                owner_of(source, strip), :, pl.ds(strip % per_owner * TILE, TILE), :
            ],
            send_sem=send_sem.at[strip, peer],
            recv_sem=recv_sem.at[strip, source],
            device_id=(peer // near, side * near + peer % near),
            device_id_type=pl.DeviceIdType.MESH,
        )

    for strip in range(strips):
        @pl.loop(0, TILE // STEP)
        def _(block):
            transform_block(grid_ref, tables_of, stage_ref, turn_ref, strip * TILE + block * STEP)

        @pl.loop(1, peers)
        def _(n):
            piece(strip, (mine + n) % peers, mine).start()

    lines = per_owner * TILE
    for part in range(2):
        own = pltpu.make_async_copy(
            stage_ref.at[pl.ds(mine * share, share), pl.ds(part * lines, lines), :],
            got_ref.at[owner_of(mine, part * per_owner)],
            own_sem.at[part],
        )
        own.start()
        own.wait()
    for strip in range(strips):
        @pl.loop(1, peers)
        def _(n):
            piece(strip, (mine + n) % peers, mine).wait_send()

        @pl.loop(1, peers)
        def _(n):
            peer = (mine + n) % peers
            piece(strip, peer, peer).wait_recv()


def column_kernel(
    x_ref, eh_ref, el_ref, wre_ref, wim_ref, fh_ref, fl_ref, out_ref, wide_ref, mid_ref, turn_ref
):
    sources, lines = x_ref.shape[0], x_ref.shape[3]

    @pl.loop(0, sources)
    def _(source):
        at = pl.ds(pl.multiple_of(source * lines, lines), lines)
        for c in range(2):
            wide_ref[c, at, :] = x_ref[source, c, 0].astype(jnp.float32)

    @pl.loop(0, TILE // 2)
    def _(half):
        for n in range(2):
            i = half * 2 + n
            cells = jnp.concatenate(
                [wide_ref[c, pl.ds(i, COARSE, stride=TILE), :] for c in range(2)], axis=0
            ).astype(jnp.bfloat16)
            middle = mm(cells, eh_ref[...], ((0,), (0,))) + mm(cells, el_ref[...], ((0,), (0,)))
            re, im = middle[:, :COARSE], middle[:, COARSE:]
            wre, wim = wre_ref[pl.ds(i, 1), :], wim_ref[pl.ds(i, 1), :]
            mid_ref[0, pl.ds(i, COARSE, stride=TILE), :] = re * wre - im * wim
            mid_ref[1, pl.ds(i, COARSE, stride=TILE), :] = re * wim + im * wre

    @pl.loop(0, COARSE // 8)
    def _(block):
        for n in range(8):
            at = pl.ds(pl.multiple_of((block * 8 + n) * TILE, TILE), TILE)
            cells = jnp.concatenate([mid_ref[c, at, :] for c in range(2)], axis=0)
            high, low = split(cells)
            result = mm(
                jnp.concatenate([fh_ref[...], fl_ref[...]], axis=0),
                jnp.concatenate([high, low], axis=0),
            )
            result = result[: 2 * TILE] + result[2 * TILE :]
            turn_ref[pl.ds(n, 2 * TILE, stride=8), :] = result
        rows = pl.ds(pl.multiple_of(block * 8, 8), 8)
        for c in range(2):
            for m in range(TILE):
                out_ref[c, rows, m * COARSE : (m + 1) * COARSE] = turn_ref[
                    (c * TILE + m) * 8 : (c * TILE + m + 1) * 8, :
                ]


def local(visibilities, owner, tile_slot, kernel_index, kernels):
    devices = lax.axis_size("grp") * lax.axis_size("dev")
    rows_here = visibilities.shape[0]
    capacity = 2 * rows_here // devices
    total = devices * capacity
    lines = GRID // devices
    width = GRID // devices
    blocks = max(1, width // COARSE)
    row_first, row_turn, row_second, col_first, col_turn, col_second = tables(blocks)

    target = owner[:, 0]
    onehot = target[:, None] == jnp.arange(devices, dtype=jnp.int32)[None, :]
    index = jnp.arange(rows_here, dtype=jnp.int32)
    before = (index[:, None] > index[None, :]).astype(jnp.bfloat16)
    ranks = mm(before, onehot.astype(jnp.bfloat16))
    rank = jnp.sum(jnp.where(onehot, ranks, 0.0), axis=1).astype(jnp.int32)
    position = target * capacity + rank
    place = (jnp.arange(total, dtype=jnp.int32)[:, None] == position[None, :]).astype(jnp.bfloat16)
    labels = jnp.stack(
        [
            tile_slot // COARSE,
            tile_slot % COARSE,
            kernel_index[:, 0],
            kernel_index[:, 1],
            jnp.ones_like(tile_slot),
        ],
        axis=1,
    ).astype(jnp.bfloat16)
    payload = jnp.concatenate(
        [
            visibilities.reshape(rows_here, 2 * VIS),
            jnp.pad(labels, ((0, 0), (0, VIS - labels.shape[1]))),
        ],
        axis=1,
    )
    sent = mm(place, payload).astype(jnp.bfloat16).reshape(devices, capacity, 3 * VIS)
    groups, owners = lax.axis_size("grp"), lax.axis_size("dev")
    copies = 2 if width >= COARSE else 1
    if copies == 2:
        other = sent.reshape(groups, 2, owners // 2, capacity, 3 * VIS)[:, ::-1]
        sent = jnp.concatenate([sent, other.reshape(sent.shape)], axis=1)
    got = lax.all_to_all(sent, AXES, split_axis=0, concat_axis=0, tiled=True)
    total = copies * total
    got = got.reshape(total, 3 * VIS)
    vis_in = got[:, : 2 * VIS].astype(jnp.float32)
    label_in = got[:, 2 * VIS : 2 * VIS + 5].astype(jnp.int32)
    part = jnp.arange(total, dtype=jnp.int32) // capacity % copies
    tile_in = (part * (lines // TILE) + label_in[:, 0]) * COARSE + label_in[:, 1]

    left = jnp.concatenate([kernels[0], kernels[0]], axis=2)
    right = jnp.swapaxes(kernels[1], 1, 2)
    empty = jnp.zeros_like(right)
    right = jnp.concatenate(
        [jnp.concatenate([right, empty], axis=2), jnp.concatenate([empty, right], axis=2)], axis=1
    )
    smem = pl.BlockSpec(memory_space=pltpu.SMEM)
    vmem = pl.BlockSpec(memory_space=pltpu.VMEM)
    field = pl.pallas_call(
        grid_kernel,
        out_shape=jax.ShapeDtypeStruct((copies * lines * COARSE, 2 * TILE), jnp.float32),
        in_specs=[smem] * 4 + [vmem] * 3,
        out_specs=vmem,
        compiler_params=pltpu.CompilerParams(vmem_limit_bytes=48 << 20),
        name="grid_cells",
    )(tile_in, label_in[:, 2], label_in[:, 3], label_in[:, 4], vis_in, left, right)
    shares = 2 * TILE // copies
    if copies == 2:
        side = lax.axis_index("dev") // (owners // 2)
        row_second = [
            lax.dynamic_index_in_dim(
                jnp.asarray(table).reshape(groups, 2, shares // groups, table.shape[1]),
                side, 1, keepdims=False,
            ).reshape(shares, table.shape[1])
            for table in row_second
        ]
    row_tables = (*row_first, *row_turn, *row_second)
    turned = pltpu.VMEM((shares * STEP, COARSE), jnp.float32)
    if copies == 2:
        columns = pl.pallas_call(
            functools.partial(send_kernel, groups, owners),
            out_shape=jax.ShapeDtypeStruct((devices, 2 * blocks, lines, COARSE), jnp.bfloat16),
            in_specs=[vmem] * 7,
            out_specs=pl.BlockSpec(memory_space=pl.ANY),
            scratch_shapes=[
                pltpu.VMEM((shares, copies * lines, COARSE), jnp.bfloat16),
                turned,
                pltpu.SemaphoreType.DMA((copies * lines // TILE, devices // copies)),
                pltpu.SemaphoreType.DMA((copies * lines // TILE, devices // copies)),
                pltpu.SemaphoreType.DMA((2,)),
            ],
            compiler_params=pltpu.CompilerParams(
                vmem_limit_bytes=54 << 20, has_side_effects=True
            ),
            name="rows_sent",
        )(field, *row_tables)
        columns = columns.reshape(devices, 2, blocks, lines, COARSE)
    else:
        half = pl.pallas_call(
            row_kernel,
            out_shape=jax.ShapeDtypeStruct((2 * TILE, lines, COARSE), jnp.bfloat16),
            in_specs=[vmem] * 7,
            out_specs=vmem,
            scratch_shapes=[turned],
            compiler_params=pltpu.CompilerParams(vmem_limit_bytes=52 << 20),
            name="rows",
        )(field, *row_tables)
        parts = COARSE // width
        half = half.reshape(TILE, 2, lines, parts, width).transpose(0, 3, 1, 2, 4)
        half = half.reshape(devices, 2, blocks, lines, width)
        columns = lax.all_to_all(half, AXES, split_axis=0, concat_axis=0, tiled=True)
        columns = jnp.pad(columns, ((0, 0),) * 4 + ((0, COARSE - width),))
    fixed = lambda table: pl.BlockSpec(table.shape, lambda b: (0,) * table.ndim)
    constants = (*col_first, *col_turn, *col_second)
    image = pl.pallas_call(
        column_kernel,
        grid=(blocks,),
        out_shape=jax.ShapeDtypeStruct((2, blocks * COARSE, GRID), jnp.float32),
        in_specs=[pl.BlockSpec((devices, 2, 1, lines, COARSE), lambda b: (0, 0, b, 0, 0))]
        + [fixed(table) for table in constants],
        out_specs=pl.BlockSpec((2, COARSE, GRID), lambda b: (0, b, 0)),
        scratch_shapes=[
            pltpu.VMEM((2, GRID, COARSE), jnp.float32),
            pltpu.VMEM((2, TILE * COARSE, COARSE), jnp.float32),
            pltpu.VMEM((2 * TILE * 8, COARSE), jnp.float32),
        ],
        compiler_params=pltpu.CompilerParams(
            dimension_semantics=("arbitrary",), vmem_limit_bytes=56 << 20
        ),
        name="columns",
    )(columns, *constants)
    return image[:, :width]


def solution(mesh):
    return jax.shard_map(
        local,
        mesh=mesh,
        in_specs=(
            P(AXES, None, None),
            P(AXES, None),
            P(AXES),
            P(AXES, None),
            P(),
        ),
        out_specs=P(None, AXES, None),
        check_vma=False,
    )
```
